32 devices in a mesh: replica: 16 (over z, x, core), shard: 2 (over y).
Axes of the slice: x: 2, y: 2, z: 4, core: 2. Of those that a mesh axis runs over, the one named last changes fastest.
Arguments:
- tokens: bfloat16 [16384, 768], P(('replica', 'shard')), may hold values from -6 to 6
- grad_output: bfloat16 [16384, 768], P(('replica', 'shard')), may hold values from -6 to 6
- w_attn: bfloat16 [2, 2304, 768], P(None, None, 'shard'), may hold values from -0.21875 to 0.21875
- w_proj: bfloat16 [2, 768, 768], P(None, None, 'shard'), may hold values from -0.875 to 0.875
- w_fc: bfloat16 [2, 3072, 768], P(None, None, 'shard'), may hold values from -0.21875 to 0.21875
- w_out: bfloat16 [2, 768, 3072], P(None, None, 'shard'), may hold values from -0.109375 to 0.109375
- ln_gain: bfloat16 [2, 2, 768], P(None, None, 'shard'), may hold values from 0.5 to 1.5
- ln_shift: bfloat16 [2, 2, 768], P(None, None, 'shard'), may hold values from -1.75 to 1.75
- biases: bfloat16 [2, 4, 768], P(None, None, 'shard'), may hold values from -1.75 to 1.75
- fc_bias: bfloat16 [2, 1, 3072], P(None, None, 'shard'), may hold values from -1.75 to 1.75
Outputs:
- output: bfloat16 [16384, 768], P(('replica', 'shard'))
- grad_tokens: bfloat16 [16384, 768], P(('replica', 'shard'))
- grad_w_attn: float32 [2, 2304, 768], P(None, None, 'shard')
- grad_w_proj: float32 [2, 768, 768], P(None, None, 'shard')
- grad_w_fc: float32 [2, 3072, 768], P(None, None, 'shard')
- grad_w_out: float32 [2, 768, 3072], P(None, None, 'shard')
- grad_ln_gain: float32 [2, 2, 768], P(None, None, 'shard')
- grad_ln_shift: float32 [2, 2, 768], P(None, None, 'shard')
- grad_biases: float32 [2, 4, 768], P(None, None, 'shard')
- grad_fc_bias: float32 [2, 1, 3072], P(None, None, 'shard')
The draws below stay inside these ranges and needn't reach their ends.
All inputs are finite; a program needn't handle non-finite values.
Results may differ from the reference program's by a relative error of at most 0.017.
Values may be sent and summed in bfloat16 or wider, within the bound.
No kernel may reach another device: no remote copies, remote signals or barrier semaphores. Data moves between devices by JAX's collectives and lax.ppermute only.
A program may use at most 320 MiB of HBM per device.

```python
import math
import jax
import jax.numpy as jnp
from jax import lax

D = 768
HEADS = 12
HEAD_DIM = 64
FF = 3072
LEN = 512
LAYERS = 2
TOKENS = 16384


def shard_levels(own_key, shape, cuts, low, top_value):
    level = 1.0
    for axis_at, parts in cuts:
        heights = jax.random.uniform(jax.random.fold_in(jax.random.fold_in(own_key, 6), axis_at), (parts,), jnp.float32, low / len(cuts), top_value / len(cuts))
        level = level * jnp.repeat(jnp.exp(heights), shape[axis_at] // parts).reshape((-1,) + (1,) * (len(shape) - 1 - axis_at))
    return level


def scatter_about(own_key, dims, width, reach, split=(), dtype=jnp.bfloat16):
    result = width * jax.random.normal(own_key, dims, jnp.float32)
    if split:
        result = result * shard_levels(own_key, dims, split, -0.22, 0.18)
    return jnp.clip(result, -reach, reach).astype(dtype)


def setup_inputs(seed: int = 0) -> dict:
    keys = jax.random.split(jax.random.key(seed), 11)
    return {
        "tokens": scatter_about(keys[0], (TOKENS, D), 1.0, 6.0, ((0, 32),)),
        "grad_output": scatter_about(keys[1], (TOKENS, D), 1.0, 6.0, ((0, 32),)),
        "w_attn": scatter_about(keys[2], (LAYERS, 3 * D, D), D ** -0.5, 0.21875, ((2, 2),)),
        "w_proj": scatter_about(keys[3], (LAYERS, D, D), (D // 16) ** -0.5, 0.875, ((2, 2),)),
        "w_fc": scatter_about(keys[4], (LAYERS, FF, D), D ** -0.5, 0.21875, ((2, 2),)),
        "w_out": scatter_about(keys[5], (LAYERS, D, FF), FF ** -0.5, 0.109375, ((2, 2),)),
        "ln_gain": jnp.clip(1.0 + 0.1 * jax.random.normal(keys[6], (LAYERS, 2, D), jnp.float32), 0.5, 1.5).astype(jnp.bfloat16),
        "ln_shift": scatter_about(keys[7], (LAYERS, 2, D), 0.3, 1.75, ((2, 2),)),
        "biases": scatter_about(keys[8], (LAYERS, 4, D), 0.3, 1.75, ((2, 2),)),
        "fc_bias": scatter_about(keys[9], (LAYERS, 1, FF), 0.3, 1.75, ((2, 2),)),
    }


@jax.custom_vjp
def low(v):
    return lax.optimization_barrier(v.astype(jnp.bfloat16)).astype(jnp.float32)

@jax.custom_vjp
def low_back(v):
    return v

def low_keep(v):
    return (low(v), None)

def low_pass(kept, grad):
    return (grad,)

def back_keep(v):
    return (v, None)

def back_low(kept, grad):
    return (low(grad),)
low.defvjp(low_keep, low_pass)
low_back.defvjp(back_keep, back_low)
highest = lax.Precision.HIGHEST
norm_eps = 1e-05
gelu_coef = 0.7978845608028654
masked_score = -1e+30

def layer_norm(stream, gain, shift):
    center = lax.optimization_barrier(jnp.mean(stream, axis=-1, keepdims=True))
    offset = stream - center
    spread = lax.optimization_barrier(jnp.mean(offset * offset, axis=-1, keepdims=True))
    return offset * lax.rsqrt(spread + norm_eps) * gain + shift

def gelu_tanh(pre_act):
    return 0.5 * pre_act * (1.0 + jnp.tanh(gelu_coef * (pre_act + 0.044715 * pre_act * pre_act * pre_act)))

def linear_map(acts, weight):
    return jnp.einsum('td,od->to', acts, weight, precision=highest)

def attend_sequence(inputs):
    queries, keys_in, values_in = inputs
    scale_factor = queries.shape[-1] ** (-0.5)
    length = queries.shape[0]
    scores = low_back(jnp.einsum('qhd,khd->hqk', queries, keys_in, precision=highest) * scale_factor)
    row_ids = lax.broadcasted_iota(jnp.int32, (length, length), 0)
    col_ids = lax.broadcasted_iota(jnp.int32, (length, length), 1)
    scores = jnp.where((col_ids <= row_ids)[None], scores, masked_score)
    row_peak = lax.optimization_barrier(jnp.max(scores, axis=-1, keepdims=True))
    expd_scores = jnp.exp(scores - row_peak)
    probs = expd_scores / lax.optimization_barrier(jnp.sum(expd_scores, axis=-1, keepdims=True))
    return jnp.einsum('hqk,khd->qhd', low(probs), values_in, precision=highest)

def one_layer(stream, params, layer_index):
    w_attn, w_proj, w_fc, w_out, ln_gain, ln_shift, biases, fc_bias = params
    rows = stream.shape[0]
    seq_count = rows // LEN
    normed = low(layer_norm(stream, ln_gain[layer_index, 0], ln_shift[layer_index, 0]))
    joined = linear_map(normed, w_attn[layer_index])
    queries = low(low_back(joined[:, :D] + biases[layer_index, 0]))
    keys_in = low(low_back(joined[:, D:2 * D]))
    values_in = low(low_back(joined[:, 2 * D:] + biases[layer_index, 1]))
    head_shape = (seq_count, LEN, HEADS, HEAD_DIM)
    mixed_out = lax.map(jax.checkpoint(attend_sequence), (queries.reshape(head_shape), keys_in.reshape(head_shape), values_in.reshape(head_shape)))
    mixed_out = low(low_back(mixed_out.reshape(rows, D)))
    middle = stream + low_back(linear_map(mixed_out, w_proj[layer_index]) + biases[layer_index, 2])
    normed_two = low(layer_norm(middle, ln_gain[layer_index, 1], ln_shift[layer_index, 1]))
    pre_act = low_back(linear_map(normed_two, w_fc[layer_index]) + fc_bias[layer_index, 0])
    hidden = low(gelu_tanh(pre_act))
    return middle + low_back(linear_map(hidden, w_out[layer_index]) + biases[layer_index, 3])

def forward(params, stream):
    for layer_index in range(LAYERS):
        stream = one_layer(stream, params, layer_index)
    return stream

def add_pair(first, second):
    return first + second

def reference(tokens, grad_output, w_attn, w_proj, w_fc, w_out, ln_gain, ln_shift, biases, fc_bias):
    params = tuple((item.astype(jnp.float32) for item in (w_attn, w_proj, w_fc, w_out, ln_gain, ln_shift, biases, fc_bias)))
    seq_total = tokens.shape[0] // LEN
    group_seqs = math.gcd(seq_total, 8)
    step_count = seq_total // group_seqs
    token_groups = tokens.astype(jnp.float32).reshape(step_count, group_seqs * LEN, D)
    grad_groups = grad_output.astype(jnp.float32).reshape(step_count, group_seqs * LEN, D)

    def scan_step(running, inputs):
        group_in, group_grad = inputs
        group_out, pull_back = jax.vjp(forward, params, group_in)
        param_grads, input_grad = pull_back(group_grad)
        running = jax.tree.map(add_pair, running, param_grads)
        return (running, (group_out.astype(jnp.bfloat16), input_grad.astype(jnp.bfloat16)))
    start_grads = tuple((jnp.zeros_like(item) for item in params))
    summed, (group_outs, group_dx) = lax.scan(scan_step, start_grads, (token_groups, grad_groups))
    return (group_outs.reshape(tokens.shape), group_dx.reshape(tokens.shape), summed[0], summed[1], summed[2], summed[3], summed[4], summed[5], summed[6], summed[7])
```

```python
import jax
import jax.numpy as jnp
from jax import lax
from jax.experimental import pallas as pl
from jax.experimental.pallas import tpu as pltpu
from jax.sharding import PartitionSpec as P

HEADS = 12
LEN = 512
BLOCK = 256
norm_eps = 1e-05
gelu_coef = 0.7978845608028654
masked_score = -1e30
f32 = jnp.float32
bf16 = jnp.bfloat16


def dot_nt(a, b):
    return lax.dot_general(a, b, (((1,), (1,)), ((), ())), preferred_element_type=f32)


def dot_nn(a, b):
    return lax.dot_general(a, b, (((1,), (0,)), ((), ())), preferred_element_type=f32)


def dot_tn(a, b):
    return lax.dot_general(a, b, (((0,), (0,)), ((), ())), preferred_element_type=f32)


def head_mask(x, j):
    lane = lax.broadcasted_iota(jnp.int32, x.shape, 1)
    keep = (lane < 64) if j == 0 else (lane >= 64)
    return jnp.where(keep, x, jnp.zeros_like(x))


def block_scores(qm, k, at):
    s = dot_nt(qm, k) * 0.125
    rows, cols = s.shape
    row = lax.broadcasted_iota(jnp.int32, (rows, cols), 0) + at
    col = lax.broadcasted_iota(jnp.int32, (rows, cols), 1)
    return jnp.where(col <= row, s, masked_score)


def attn_fwd_kernel(q_ref, k_ref, v_ref, o_ref, lse_ref):
    for i in range(LEN // BLOCK):
        at = i * BLOCK
        top = at + BLOCK
        q = q_ref[at:top, :]
        k = k_ref[:top, :]
        v = v_ref[:top, :]
        out = None
        lses = []
        for j in range(2):
            s = block_scores(head_mask(q, j), k, at)
            peak = jnp.max(s, axis=-1, keepdims=True)
            e = jnp.exp(s - peak)
            total = jnp.sum(e, axis=-1, keepdims=True)
            p = (e * (1.0 / total)).astype(bf16)
            part = dot_nn(p, head_mask(v, j))
            out = part if out is None else out + part
            lses.append(jnp.broadcast_to(peak + jnp.log(total), (BLOCK, 64)))
        o_ref[at:top, :] = out.astype(bf16)
        lse_ref[at:top, :] = jnp.concatenate(lses, axis=1)


def attn_fwd(c):
    pairs = HEADS // 2
    width = c.shape[1] // 3
    seqs = c.shape[0] // LEN
    return pl.pallas_call(
        attn_fwd_kernel,
        grid=(seqs, pairs),
        in_specs=[
            pl.BlockSpec((LEN, 128), lambda t, h: (t, h)),
            pl.BlockSpec((LEN, 128), lambda t, h: (t, h + pairs)),
            pl.BlockSpec((LEN, 128), lambda t, h: (t, h + 2 * pairs)),
        ],
        out_specs=[
            pl.BlockSpec((LEN, 128), lambda t, h: (t, h)),
            pl.BlockSpec((LEN, 128), lambda t, h: (t, h)),
        ],
        out_shape=[
            jax.ShapeDtypeStruct((c.shape[0], width), bf16),
            jax.ShapeDtypeStruct((c.shape[0], width), f32),
        ],
        cost_estimate=pl.CostEstimate(
            flops=12 * LEN * LEN * 64 * 4, bytes_accessed=6 << 20, transcendentals=12 * LEN * LEN
        ),
        name="attn_fwd",
    )(c, c, c)


def attn_bwd_kernel(q_ref, k_ref, v_ref, lse_ref, do_ref, dc_ref, dk_acc, dv_acc):
    h = pl.program_id(1)
    dk_acc[...] = jnp.zeros_like(dk_acc)
    dv_acc[...] = jnp.zeros_like(dv_acc)
    for i in range(LEN // BLOCK):
        at = i * BLOCK
        top = at + BLOCK
        q = q_ref[at:top, :]
        do = do_ref[at:top, :]
        k = k_ref[:top, :]
        v = v_ref[:top, :]
        dq = None
        dk = None
        dv = None
        for j in range(2):
            qm = head_mask(q, j)
            dom = head_mask(do, j)
            s = block_scores(qm, k, at)
            p = jnp.exp(s - lse_ref[at:top, 64 * j : 64 * j + 1])
            dp = dot_nt(dom, v)
            inner = jnp.sum(dp * p, axis=-1, keepdims=True)
            ds = (p * (dp - inner)).astype(bf16)
            dq_j = dot_nn(ds, head_mask(k, j))
            dk_j = dot_tn(ds, qm)
            dv_j = dot_tn(p.astype(bf16), dom)
            dq = dq_j if dq is None else dq + dq_j
            dk = dk_j if dk is None else dk + dk_j
            dv = dv_j if dv is None else dv + dv_j
        dc_ref[at:top, pl.ds(pl.multiple_of(h * 128, 128), 128)] = (dq * 0.125).astype(bf16)
        dk_acc[:top, :] += dk
        dv_acc[:top, :] += dv
    width = dc_ref.shape[1] // 3
    dc_ref[:, pl.ds(pl.multiple_of(width + h * 128, 128), 128)] = (dk_acc[...] * 0.125).astype(bf16)
    dc_ref[:, pl.ds(pl.multiple_of(2 * width + h * 128, 128), 128)] = dv_acc[...].astype(bf16)


def attn_bwd(c, lse, do):
    pairs = HEADS // 2
    seqs = c.shape[0] // LEN
    return pl.pallas_call(
        attn_bwd_kernel,
        grid=(seqs, pairs),
        in_specs=[
            pl.BlockSpec((LEN, 128), lambda t, h: (t, h)),
            pl.BlockSpec((LEN, 128), lambda t, h: (t, h + pairs)),
            pl.BlockSpec((LEN, 128), lambda t, h: (t, h + 2 * pairs)),
            pl.BlockSpec((LEN, 128), lambda t, h: (t, h)),
            pl.BlockSpec((LEN, 128), lambda t, h: (t, h)),
        ],
        out_specs=pl.BlockSpec((LEN, c.shape[1]), lambda t, h: (t, 0)),
        out_shape=jax.ShapeDtypeStruct(c.shape, bf16),
        scratch_shapes=[pltpu.VMEM((LEN, 128), f32), pltpu.VMEM((LEN, 128), f32)],
        cost_estimate=pl.CostEstimate(
            flops=12 * LEN * LEN * 64 * 10, bytes_accessed=8 << 20, transcendentals=12 * LEN * LEN
        ),
        name="attn_bwd",
    )(c, c, c, lse, do)


def wgrad_kernel(at_ref, a_ref, ar_ref, bk_ref, bkr_ref, bs_ref, bsr_ref, keep_ref, send_ref):
    a = a_ref[...]
    ar = ar_ref[...]
    keep_ref[...] = (dot_tn(a, bk_ref[...]) + dot_tn(ar, bkr_ref[...])).astype(bf16)
    send_ref[...] = (dot_tn(a, bs_ref[...]) + dot_tn(ar, bsr_ref[...])).astype(bf16)


def wgrad(at, a, a_in, b, b_in, tn, tc):
    tokens = a.shape[0]
    rows = a.shape[1] // 2
    cols = b.shape[1] // 2
    nt = rows // tn
    ct = cols // tc
    grid_spec = pltpu.PrefetchScalarGridSpec(
        num_scalar_prefetch=1,
        grid=(nt, ct),
        in_specs=[
            pl.BlockSpec((tokens, tn), lambda i, j, s: (0, s[0] * nt + i)),
            pl.BlockSpec((tokens, tn), lambda i, j, s: (0, i)),
            pl.BlockSpec((tokens, tc), lambda i, j, s: (0, s[1] * ct + j)),
            pl.BlockSpec((tokens, tc), lambda i, j, s: (0, s[1] * ct + j)),
            pl.BlockSpec((tokens, tc), lambda i, j, s: (0, (1 - s[1]) * ct + j)),
            pl.BlockSpec((tokens, tc), lambda i, j, s: (0, (1 - s[1]) * ct + j)),
        ],
        out_specs=[
            pl.BlockSpec((tn, tc), lambda i, j, s: (i, j)),
            pl.BlockSpec((tn, tc), lambda i, j, s: (i, j)),
        ],
    )
    return pl.pallas_call(
        wgrad_kernel,
        grid_spec=grid_spec,
        out_shape=[jax.ShapeDtypeStruct((rows, cols), bf16)] * 2,
        cost_estimate=pl.CostEstimate(
            flops=8 * tokens * rows * cols,
            bytes_accessed=2 * tokens * (2 * rows + 4 * cols) + 4 * rows * cols,
            transcendentals=0,
        ),
        name="wgrad",
    )(at, a, a_in, b, b_in, b, b_in)


def layer_norm(stream, gain, shift):
    center = jnp.mean(stream, axis=-1, keepdims=True)
    offset = stream - center
    spread = jnp.mean(offset * offset, axis=-1, keepdims=True)
    scale = lax.rsqrt(spread + norm_eps)
    return (offset * scale * gain + shift).astype(bf16), center, scale


def layer_norm_back(stream, center, scale, gain, u):
    x = (stream - center) * scale
    gu = gain * u
    back = scale * (gu - jnp.mean(gu, axis=-1, keepdims=True) - x * jnp.mean(gu * x, axis=-1, keepdims=True))
    return back, jnp.sum(u * x, axis=0), jnp.sum(u, axis=0)


def gelu_tanh(pre):
    return 0.5 * pre * (1.0 + jnp.tanh(gelu_coef * (pre + 0.044715 * pre * pre * pre)))


def gelu_slope(pre):
    t = jnp.tanh(gelu_coef * (pre + 0.044715 * pre * pre * pre))
    return 0.5 * (1.0 + t) + 0.5 * pre * (1.0 - t * t) * gelu_coef * (1.0 + 3.0 * 0.044715 * pre * pre)


def column_sum(x):
    return jnp.sum(x.astype(f32), axis=0)


def solution(mesh):
    replicas = mesh.shape["replica"]
    levels = replicas.bit_length() - 1
    assert replicas == 1 << levels and levels >= 2

    def flip(x, bit):
        return lax.ppermute(x, "replica", [(i, i ^ (1 << bit)) for i in range(replicas)])

    def across(x):
        return lax.ppermute(x, "shard", [(0, 1), (1, 0)])

    def on_device(tokens, grad_output, w_attn, w_proj, w_fc, w_out, ln_gain, ln_shift, biases, fc_bias):
        place = lax.axis_index("replica")
        side = lax.axis_index("shard")
        bits = [(place >> b) & 1 for b in range(levels)]
        core = bits[0]
        layers = w_attn.shape[0]
        half_d = w_attn.shape[2]
        width = 2 * half_d
        at = jnp.stack([core, side]).astype(jnp.int32)

        def gather(w):
            rows, cols = w.shape
            quarter = rows // 4
            own = core * 2 + bits[1]
            q00 = across(lax.dynamic_slice_in_dim(w, own * quarter, quarter, 0))
            q01 = flip(q00, 1)
            q10 = flip(q00, 0)
            q11 = flip(q01, 0)
            full = jnp.zeros((rows, 2 * cols), bf16)
            full = lax.dynamic_update_slice(full, w, (0, side * cols))
            for piece, where in (
                (q00, own),
                (q01, core * 2 + 1 - bits[1]),
                (q10, (1 - core) * 2 + bits[1]),
                (q11, (1 - core) * 2 + 1 - bits[1]),
            ):
                full = lax.dynamic_update_slice(full, piece, (where * quarter, (1 - side) * cols))
            return full

        small = jnp.concatenate(
            [
                ln_gain.reshape(-1, half_d),
                ln_shift.reshape(-1, half_d),
                biases.reshape(-1, half_d),
                fc_bias.reshape(-1, half_d),
            ]
        )
        small_in = across(small)
        low = jnp.where(side == 0, small, small_in)
        high = jnp.where(side == 0, small_in, small)
        norm_rows = 2 * layers

        def take(start, count):
            return jnp.concatenate([low[start : start + count], high[start : start + count]], axis=1)

        gains = take(0, norm_rows).reshape(layers, 2, width).astype(f32)
        shifts = take(norm_rows, norm_rows).reshape(layers, 2, width).astype(f32)
        bias = take(2 * norm_rows, 4 * layers).reshape(layers, 4, width).astype(f32)
        ff_half = fc_bias.shape[2]
        ff_rows = ff_half // half_d
        ff_at = 2 * norm_rows + 4 * layers
        ff_bias = jnp.concatenate(
            [
                low[ff_at : ff_at + layers * ff_rows].reshape(layers, ff_half),
                high[ff_at : ff_at + layers * ff_rows].reshape(layers, ff_half),
            ],
            axis=1,
        ).astype(f32)

        weights = [[gather(w[n]) for w in (w_attn, w_proj, w_fc, w_out)] for n in range(layers)]

        stream = tokens.astype(f32)
        saved = []
        for n in range(layers):
            wa, wp, wf, wo = weights[n]
            n1, mean1, scale1 = layer_norm(stream, gains[n, 0], shifts[n, 0])
            row = jnp.concatenate([bias[n, 0], jnp.zeros((width,), f32), bias[n, 1]])
            c = (dot_nt(n1, wa) + row).astype(bf16)
            o, lse = attn_fwd(c)
            mid = stream + dot_nt(o, wp) + bias[n, 2]
            n2, mean2, scale2 = layer_norm(mid, gains[n, 1], shifts[n, 1])
            pre = dot_nt(n2, wf) + ff_bias[n]
            act = gelu_tanh(pre).astype(bf16)
            out = mid + dot_nt(act, wo) + bias[n, 3]
            swapped = [flip(x, 0) for x in (n1, o, n2, act)]
            saved.append((stream, n1, mean1, scale1, c, o, lse, mid, n2, mean2, scale2, pre, act, swapped))
            stream = out
        output = stream.astype(bf16)

        def swap_half(x):
            half = x.shape[1] // 2
            return flip(lax.dynamic_slice_in_dim(x, (1 - core) * half, half, 1), 0)

        def reduce_all(keep, send):
            sums = keep.astype(f32) + across(send).astype(f32)
            for b in range(1, levels):
                half = sums.shape[0] // 2
                theirs = lax.dynamic_slice_in_dim(sums, (1 - bits[b]) * half, half, 0).astype(bf16)
                mine = lax.dynamic_slice_in_dim(sums, bits[b] * half, half, 0)
                sums = mine + flip(theirs, b).astype(f32)
            done = sums.astype(bf16)
            for b in reversed(range(levels)):
                other = flip(done, b)
                first = jnp.where(bits[b] == 0, done, other)
                second = jnp.where(bits[b] == 0, other, done)
                done = jnp.concatenate([first, second])
            return done

        def reduce_small(vector):
            mine = jnp.where(side == 0, vector[0], vector[1])
            theirs = jnp.where(side == 0, vector[1], vector[0])
            total = mine + across(theirs)
            for b in range(levels):
                total = total + flip(total, b)
            return total

        grad = grad_output.astype(f32)
        results = [None] * layers
        for n in reversed(range(layers)):
            wa, wp, wf, wo = weights[n]
            stream, n1, mean1, scale1, c, o, lse, mid, n2, mean2, scale2, pre, act, swapped = saved[n]
            n1_in, o_in, n2_in, act_in = swapped
            dm = grad.astype(bf16)
            keep_out = wgrad(at, dm, swap_half(dm), act, act_in, 384, 384)
            dpre = (dot_nn(dm, wo) * gelu_slope(pre)).astype(bf16)
            keep_fc = wgrad(at, dpre, swap_half(dpre), n2, n2_in, 384, 384)
            back2, gain2, shift2 = layer_norm_back(mid, mean2, scale2, gains[n, 1], dot_nn(dpre, wf))
            g1 = grad + back2
            da = g1.astype(bf16)
            keep_proj = wgrad(at, da, swap_half(da), o, o_in, 384, 384)
            do = dot_nn(da, wp).astype(bf16)
            dc = attn_bwd(c, lse, do)
            keep_attn = wgrad(at, dc, swap_half(dc), n1, n1_in, 384, 384)
            back1, gain1, shift1 = layer_norm_back(stream, mean1, scale1, gains[n, 0], dot_nn(dc, wa))
            sum_c = column_sum(dc)
            vectors = [
                gain1,
                gain2,
                shift1,
                shift2,
                sum_c[:width],
                sum_c[2 * width :],
                column_sum(da),
                column_sum(dm),
                column_sum(dpre),
            ]
            grad = g1 + back1
            packed = jnp.concatenate([v.reshape(2, -1) for v in vectors], axis=1)
            tiny = reduce_small(packed)
            results[n] = (
                reduce_all(*keep_attn).astype(f32),
                reduce_all(*keep_proj).astype(f32),
                reduce_all(*keep_fc).astype(f32),
                reduce_all(*keep_out).astype(f32),
                tiny[: 2 * half_d].reshape(2, half_d),
                tiny[2 * half_d : 4 * half_d].reshape(2, half_d),
                tiny[4 * half_d : 8 * half_d].reshape(4, half_d),
                tiny[8 * half_d :].reshape(1, -1),
            )
        stacked = [jnp.stack([results[n][m] for n in range(layers)]) for m in range(8)]
        return (output, grad.astype(bf16), *stacked)

    token_spec = P(("replica", "shard"), None)
    weight_spec = P(None, None, "shard")
    return jax.shard_map(
        on_device,
        mesh=mesh,
        in_specs=(token_spec, token_spec) + (weight_spec,) * 8,
        out_specs=(token_spec, token_spec) + (weight_spec,) * 8,
        check_vma=False,
    )
```
